256 devices in a mesh: dp: 8 (over z), seq: 32 (over y, x, core).
Axes of the slice: x: 4, y: 4, z: 8, core: 2. Of those that a mesh axis runs over, the one named last changes fastest.
Arguments:
- queries: bfloat16 [256, 2, 128, 4096], P(('dp', 'seq')), parts along dimension 0, may hold values from -6 to 6
- key_heads: bfloat16 [256, 2, 128, 512], P(('dp', 'seq')), parts along dimension 0, may hold values from -6 to 6
- value_heads: bfloat16 [256, 2, 128, 512], P(('dp', 'seq')), parts along dimension 0, may hold values from -6 to 6
- out_grad: bfloat16 [256, 2, 128, 4096], P(('dp', 'seq')), parts along dimension 0, may hold values from -6 to 6
- doc_lengths: int32 [256], P('dp'), parts along dimension 0, may hold values from 1 to 384, 8192 in all
- block_reach: int32 [512], P('dp'), parts along dimension 0, may hold values from 0 to 3, as said below
Outputs:
- attended: bfloat16 [256, 2, 128, 4096], P(('dp', 'seq')), parts along dimension 0
- query_grad: bfloat16 [256, 2, 128, 4096], P(('dp', 'seq')), parts along dimension 0
- key_grad: bfloat16 [256, 2, 128, 512], P(('dp', 'seq')), parts along dimension 0
- value_grad: bfloat16 [256, 2, 128, 512], P(('dp', 'seq')), parts along dimension 0
The draws below stay inside these ranges and needn't reach their ends.
There are 8 independent parts, one for each index of `dp`. The reference program is written for one: setup_inputs(seed, part) draws one part's arguments, and reference() takes and returns one part's arrays. A program takes and returns all parts, laid end to end along the dimension named above; each array names one. Nothing has to cross between parts.
Inputs may be any that keep to these rules, and one draw needn't show every extreme that they name: doc_lengths are positive, sum to 8192, and the longest is exactly 384. `block_reach`: the value 4 - 1 occurs in every draw.
All inputs are finite; a program needn't handle non-finite values.
Results may differ from the reference program's by a relative error of at most 0.025.
Values may be sent and summed in bfloat16 or wider, within the bound.
No kernel may reach another device: no remote copies, remote signals or barrier semaphores. Data moves between devices by JAX's collectives and lax.ppermute only.
A program may use at most 128 MiB of HBM per device.

```python
import math
import jax
import jax.numpy as jnp
import numpy as np
from jax import lax

BLOCK_TOKENS = 128
QUERY_HEADS = 32
KEY_VALUE_HEADS = 4
HEAD_SIZE = 128
WIN = 4
QW = 4096
KVW = 512
MIRROR_PAIRS = 32
BLOCKS = 64
SEQUENCE_TOKENS = 8192
DOCS = 32
MOSTLEN = 384


def sampled_pair_blocks(ordered):
    half_blocks = ordered.shape[0] // 2
    return jnp.stack([ordered[:half_blocks], ordered[half_blocks:][::-1]], axis=1)


def draw_queries(key, part):
    value_rows = jax.random.truncated_normal(jax.random.fold_in(key, 11), -6.0, 6.0, (SEQUENCE_TOKENS, QUERY_HEADS, HEAD_SIZE), jnp.float32)
    return sampled_pair_blocks(value_rows.reshape(2 * MIRROR_PAIRS, BLOCK_TOKENS, QUERY_HEADS * HEAD_SIZE)).astype(jnp.bfloat16)


def draw_key_heads(key, part):
    value_rows = jax.random.truncated_normal(jax.random.fold_in(key, 12), -6.0, 6.0, (SEQUENCE_TOKENS, KEY_VALUE_HEADS, HEAD_SIZE), jnp.float32)
    return sampled_pair_blocks(value_rows.reshape(2 * MIRROR_PAIRS, BLOCK_TOKENS, KEY_VALUE_HEADS * HEAD_SIZE)).astype(jnp.bfloat16)


def draw_block_reach(key, part):
    levels = jax.random.randint(jax.random.fold_in(key, 21), (BLOCKS,), 0, WIN)
    chosen_block = jax.random.randint(jax.random.fold_in(key, 22), (), 0, BLOCKS)
    return jnp.where(jnp.arange(BLOCKS) == chosen_block, WIN - 1, levels).astype(jnp.int32)


def shard_levels(rng, extent, cuts, smallest, high):
    loudness, own = 1.0, jax.random.fold_in(rng, 6)
    for dim, shards_of in cuts:
        draws = jnp.exp(jax.random.uniform(jax.random.fold_in(own, dim), (shards_of,), jnp.float32, smallest / len(cuts), high / len(cuts)))
        loudness = loudness * jnp.repeat(draws, extent[dim] // shards_of).reshape([-1 if axis == dim else 1 for axis in range(len(extent))])
    return loudness


def length_profile(count, total, reach, skew):
    portions = [(1 << 20) // math.isqrt(grade ** skew) + 1 for grade in range(2, count + 1)]
    spare, given = total - reach - (count - 1), [1] * (count - 1)
    while spare > 0:
        movable = [i for i in range(count - 1) if given[i] < reach]
        whole, left = sum([portions[i] for i in movable]), spare
        for i in movable:
            more = min(reach - given[i], max(1, left * portions[i] // whole), spare)
            given[i] = given[i] + more
            spare = spare - more
    return np.array([reach] + given)


def uneven(key, count, total, reach, skew):
    if count == 2:
        one = jax.random.randint(key, (), max(1, total - reach), min(reach, total - 1) + 1)
        return jnp.stack([one, total - one])
    sizes = jnp.asarray(length_profile(count, total, reach, skew), jnp.int32)
    couples = (count - 1) // 2
    source_of, taker = sizes[1:1 + 2 * couples:2], sizes[2:2 + 2 * couples:2]
    room = jnp.minimum(source_of - 1, reach - taker)
    shifted = jax.random.randint(jax.random.fold_in(key, 1), (couples,), 0, 1 << 20) % (room + 1)
    sizes = sizes.at[1:1 + 2 * couples:2].set(source_of - shifted).at[2:2 + 2 * couples:2].set(taker + shifted)
    return sizes[jax.random.permutation(jax.random.fold_in(key, 2), count)]


def bell_draw(stream_key, shape, deviation, reach, cuts=(), kind=jnp.bfloat16):
    gain = shard_levels(stream_key, shape, cuts, -0.22, 0.18) if cuts else 1.0
    entries = jax.random.normal(stream_key, shape, jnp.float32) * deviation * gain
    return jnp.minimum(jnp.maximum(entries, -reach), reach).astype(kind)


def setup_inputs(seed: int = 0, part: int = 0) -> dict:
    key_list = jax.random.split(jax.random.key(seed), 7)
    part_splits = jax.random.split(jax.random.fold_in(key_list[6], part), 7)
    return {
        "queries": draw_queries(jax.random.fold_in(jax.random.fold_in(key_list[6], part), 71), part),
        "key_heads": draw_key_heads(jax.random.fold_in(jax.random.fold_in(key_list[6], part), 71), part),
        "value_heads": bell_draw(part_splits[2], (MIRROR_PAIRS, 2, BLOCK_TOKENS, KVW), 1.0, 6.0, ((0, 32),)),
        "out_grad": bell_draw(part_splits[3], (MIRROR_PAIRS, 2, BLOCK_TOKENS, QW), 1.0, 6.0, ((0, 32),)),
        "doc_lengths": uneven(part_splits[4], DOCS, SEQUENCE_TOKENS, MOSTLEN, 2).astype(jnp.int32),
        "block_reach": draw_block_reach(jax.random.fold_in(jax.random.fold_in(key_list[6], part), 71), part),
    }


masked_fill = -1e30


def to_sequence(paired):
    return jnp.concatenate([paired[:, 0], paired[::-1, 1]], axis=0)


def to_pairs(ordered):
    half_blocks = ordered.shape[0] // 2
    return jnp.stack([ordered[:half_blocks], ordered[half_blocks:][::-1]], axis=1)


def doc_index(positions, doc_ends):
    return jnp.sum((positions[:, None] >= doc_ends[None, :]).astype(jnp.int32), axis=1)


def attend(queries_blk, grads_blk, key_window, value_window, first_key, block_index, reach_now, doc_ends):
    block_rows = queries_blk.shape[0]
    key_rows = key_window.shape[0]
    kv_width = key_window.shape[1]
    heads_kv = kv_width // HEAD_SIZE
    group_size = queries_blk.shape[1] // kv_width
    score_scale = HEAD_SIZE ** -0.5
    q_four = queries_blk.reshape(block_rows, heads_kv, group_size, HEAD_SIZE).astype(jnp.float32)
    g_four = grads_blk.reshape(block_rows, heads_kv, group_size, HEAD_SIZE).astype(jnp.float32)
    k_three = key_window.reshape(key_rows, heads_kv, HEAD_SIZE).astype(jnp.float32)
    v_three = value_window.reshape(key_rows, heads_kv, HEAD_SIZE).astype(jnp.float32)
    query_pos = block_index * block_rows + jnp.arange(block_rows, dtype=jnp.int32)
    key_pos = first_key + jnp.arange(key_rows, dtype=jnp.int32)
    allowed = (key_pos[None, :] <= query_pos[:, None]) & (key_pos[None, :] >= 0)
    allowed = allowed & (doc_index(key_pos, doc_ends)[None, :] == doc_index(query_pos, doc_ends)[:, None])
    allowed = allowed & (key_pos[None, :] // block_rows >= block_index - reach_now)
    scores = jnp.einsum("tkgd,skd->kgts", q_four, k_three) * score_scale
    masked = jnp.where(allowed, scores, masked_fill)
    row_max = jnp.max(masked, axis=-1, keepdims=True)
    row_sum = jnp.sum(jnp.exp(masked - row_max), axis=-1, keepdims=True)
    log_total = row_max + jnp.log(row_sum)
    weights = jnp.exp(masked - log_total)
    weights_low = weights.astype(jnp.bfloat16)
    attended = jnp.einsum("kgts,skd->tkgd", weights_low.astype(jnp.float32), v_three).astype(jnp.bfloat16)
    row_delta = jnp.einsum("tkgd,tkgd->kgt", g_four, attended.astype(jnp.float32))
    weight_grad = jnp.einsum("tkgd,skd->kgts", g_four, v_three)
    score_grad = (weights * (weight_grad - row_delta[..., None]) * score_scale).astype(jnp.bfloat16)
    query_grad = jnp.einsum("kgts,skd->tkgd", score_grad.astype(jnp.float32), k_three).astype(jnp.bfloat16)
    key_part = jnp.einsum("kgts,tkgd->skd", score_grad.astype(jnp.float32), q_four)
    value_part = jnp.einsum("kgts,tkgd->skd", weights_low.astype(jnp.float32), g_four)
    return (attended.reshape(block_rows, -1), query_grad.reshape(block_rows, -1),
            key_part.reshape(key_rows, kv_width), value_part.reshape(key_rows, kv_width))


def reference(queries, key_heads, value_heads, out_grad, doc_lengths, block_reach):
    doc_ends = jnp.cumsum(doc_lengths).astype(jnp.int32)
    query_seq = to_sequence(queries)
    grad_seq = to_sequence(out_grad)
    key_seq = to_sequence(key_heads)
    value_seq = to_sequence(value_heads)
    kv_width = key_seq.shape[-1]
    padding = jnp.zeros((WIN - 1, BLOCK_TOKENS, kv_width), key_seq.dtype)
    key_padded = jnp.concatenate([padding, key_seq], axis=0)
    value_padded = jnp.concatenate([padding, value_seq], axis=0)

    def one_block(block_index):
        key_window = lax.dynamic_slice_in_dim(key_padded, block_index, WIN, 0).reshape(WIN * BLOCK_TOKENS, kv_width)
        value_window = lax.dynamic_slice_in_dim(value_padded, block_index, WIN, 0).reshape(WIN * BLOCK_TOKENS, kv_width)
        reach_now = lax.dynamic_index_in_dim(block_reach, block_index, keepdims=False)
        queries_blk = lax.dynamic_index_in_dim(query_seq, block_index, keepdims=False)
        grads_blk = lax.dynamic_index_in_dim(grad_seq, block_index, keepdims=False)
        return attend(queries_blk, grads_blk, key_window, value_window,
                      (block_index - WIN + 1) * BLOCK_TOKENS, block_index, reach_now, doc_ends)

    block_ids = jnp.arange(2 * MIRROR_PAIRS, dtype=jnp.int32)
    attended, query_grad, key_parts, value_parts = lax.map(one_block, block_ids)
    key_parts = key_parts.reshape(2 * MIRROR_PAIRS, WIN, BLOCK_TOKENS, kv_width)
    value_parts = value_parts.reshape(2 * MIRROR_PAIRS, WIN, BLOCK_TOKENS, kv_width)
    key_total = jnp.zeros((2 * MIRROR_PAIRS + WIN - 1, BLOCK_TOKENS, kv_width), jnp.float32)
    value_total = jnp.zeros((2 * MIRROR_PAIRS + WIN - 1, BLOCK_TOKENS, kv_width), jnp.float32)
    for offset in range(WIN):
        key_total = key_total.at[offset:offset + 2 * MIRROR_PAIRS].add(key_parts[:, offset])
        value_total = value_total.at[offset:offset + 2 * MIRROR_PAIRS].add(value_parts[:, offset])
    key_grad = to_pairs(key_total[WIN - 1:].astype(jnp.bfloat16))
    value_grad = to_pairs(value_total[WIN - 1:].astype(jnp.bfloat16))
    return (to_pairs(attended), to_pairs(query_grad), key_grad, value_grad)
```

```python
import jax
import jax.numpy as jnp
from jax import lax
from jax.experimental import pallas as pl
from jax.experimental.pallas import tpu as pltpu
from jax.sharding import PartitionSpec as P

HEAD = 128
WIN = 4
LOG2E = 1.4426950408889634
MASKED = -1e30
NT = (((1,), (1,)), ((), ()))
TN = (((0,), (0,)), ((), ()))


def row_bias(info_ref, lens_ref, reach_ref, edge, rows):
    block = info_ref[2 + edge]
    reach = reach_ref[block]
    t = block * rows + lax.broadcasted_iota(jnp.int32, (rows, HEAD), 0)
    first = jnp.maximum((block - reach) * rows, 0)
    lo = jnp.zeros((rows, HEAD), jnp.int32) + first

    def one_doc(i, carry):
        lo, end = carry
        end = end + lens_ref[i]
        return jnp.where(end <= t, jnp.maximum(lo, end), lo), end

    lo, _ = lax.fori_loop(0, lens_ref.shape[0], one_doc, (lo, jnp.int32(0)), unroll=True)
    parts = []
    for w in range(WIN):
        s = (block - (WIN - 1) + w) * rows + lax.broadcasted_iota(jnp.int32, (rows, rows), 1)
        ok = (s <= t) & (s >= lo)
        parts.append(jnp.where(ok, 0.0, MASKED).astype(jnp.float32))
    return jnp.concatenate(parts, axis=1)


def attend_kernel(edge, aliased, info_ref, lens_ref, reach_ref, q_ref, g_ref, *refs):
    if aliased:
        refs = refs[:8] + refs[10:]
    (k3, v3, k2, v2, k1, v1, k0, v0,
     att_ref, dq_ref, far_ref, near_ref, bias_ref, p_all, ds_all, qs_all, gs_all) = refs
    rows = q_ref.shape[2]
    heads = q_ref.shape[3] // HEAD
    scale = HEAD ** -0.5
    c2 = scale * LOG2E

    @pl.when(pl.program_id(0) == 0)
    def _():
        bias_ref[...] = row_bias(info_ref, lens_ref, reach_ref, edge, rows)

    flat = lambda r: r[...].reshape(rows, HEAD)
    keys = jnp.concatenate([flat(k3), flat(k2), flat(k1), flat(k0)], axis=0)
    vals = jnp.concatenate([flat(v3), flat(v2), flat(v1), flat(v0)], axis=0)
    ones = jnp.ones((WIN * rows, HEAD), jnp.bfloat16)
    vaug = jnp.concatenate([vals, ones], axis=1)
    for h in range(heads):
        cols = slice(h * HEAD, (h + 1) * HEAD)
        band = slice(h * rows, (h + 1) * rows)
        qh = q_ref[0, 0, :, cols]
        gh = g_ref[0, 0, :, cols]
        s = lax.dot_general(qh, keys, NT, preferred_element_type=jnp.float32) + bias_ref[...]
        m = jnp.max(s, axis=1, keepdims=True)
        p = jnp.exp2((s - m) * c2)
        pb = p.astype(jnp.bfloat16)
        p_all[band, :] = pb
        o = jnp.dot(pb, vaug, preferred_element_type=jnp.float32)
        inv = 1.0 / o[:, HEAD:]
        att = (o[:, :HEAD] * inv).astype(jnp.bfloat16)
        att_ref[0, 0, :, cols] = att
        g32 = gh.astype(jnp.float32)
        delta = jnp.sum(g32 * att.astype(jnp.float32), axis=1, keepdims=True)
        dp = lax.dot_general(gh, vals, NT, preferred_element_type=jnp.float32)
        ds = (p * (dp - delta)).astype(jnp.bfloat16)
        ds_all[band, :] = ds
        invs = inv * scale
        gs_all[band, :] = (g32 * inv).astype(jnp.bfloat16)
        qs_all[band, :] = (qh.astype(jnp.float32) * invs).astype(jnp.bfloat16)
        dq = jnp.dot(ds, keys, preferred_element_type=jnp.float32) * invs
        dq_ref[0, 0, :, cols] = dq.astype(jnp.bfloat16)
    dk = lax.dot_general(ds_all[...], qs_all[...], TN, preferred_element_type=jnp.float32)
    dv = lax.dot_general(p_all[...], gs_all[...], TN, preferred_element_type=jnp.float32)
    split = (WIN - 1) * rows
    far_ref[0] = dk[:split].astype(jnp.bfloat16).reshape(far_ref.shape[1:])
    far_ref[1] = dv[:split].astype(jnp.bfloat16).reshape(far_ref.shape[1:])
    near_ref[0] = dk[split:]
    near_ref[1] = dv[split:]


def attend(edge, info, lens, reach, queries, grads, blocks, att=None, dq=None):
    rows = queries.shape[2]
    width = queries.shape[3]
    kvw = blocks[0][0].shape[-1]
    steps = kvw // HEAD
    group = width // kvw * HEAD
    slot = lambda info: info[edge]
    wide = pl.BlockSpec((1, 1, rows, group), lambda j, info, *_: (0, slot(info), 0, j))
    in_specs = [wide, wide]
    operands = [queries, grads]
    for array, index in blocks:
        for half in (0, 1):
            if index is None:
                pick = lambda j, info, *_, half=half: (half, slot(info), 0, j)
            else:
                pick = lambda j, info, *_, half=half, index=index: (half, index, 0, j)
            in_specs.append(pl.BlockSpec((1, 1, rows, HEAD), pick))
            operands.append(array)
    aliases = {}
    if att is not None:
        aliases = {3 + len(operands): 0, 4 + len(operands): 1}
        in_specs += [pl.BlockSpec(memory_space=pl.ANY)] * 2
        operands += [att, dq]
    bf = jnp.bfloat16
    out_shape = (
        jax.ShapeDtypeStruct(queries.shape, bf),
        jax.ShapeDtypeStruct(queries.shape, bf),
        jax.ShapeDtypeStruct((2, WIN - 1, rows, kvw), bf),
        jax.ShapeDtypeStruct((2, rows, kvw), jnp.float32),
    )
    out_specs = (
        wide,
        wide,
        pl.BlockSpec((2, WIN - 1, rows, HEAD), lambda j, *_: (0, 0, 0, j)),
        pl.BlockSpec((2, rows, HEAD), lambda j, *_: (0, 0, j)),
    )
    heads = group // HEAD
    tall = heads * rows
    kernel = lambda *refs: attend_kernel(edge, att is not None, *refs)
    return pl.pallas_call(
        kernel,
        out_shape=out_shape,
        grid_spec=pltpu.PrefetchScalarGridSpec(
            num_scalar_prefetch=3,
            grid=(steps,),
            in_specs=in_specs,
            out_specs=out_specs,
            scratch_shapes=[
                pltpu.VMEM((rows, WIN * rows), jnp.float32),
                pltpu.VMEM((tall, WIN * rows), bf),
                pltpu.VMEM((tall, WIN * rows), bf),
                pltpu.VMEM((tall, HEAD), bf),
                pltpu.VMEM((tall, HEAD), bf),
            ],
        ),
        input_output_aliases=aliases,
        name="attend_edge" if edge else "attend_inner",
    )(info, lens, reach, *operands)


def routes(n):
    chips = n // 2
    swap = [(i, i ^ 1) for i in range(n)]
    step = [(2 * c, 2 * c + 2) for c in range(chips - 1)] + [(n - 2, n - 1)]
    step += [(2 * c + 1, 2 * c - 1) for c in range(1, chips)]
    far = [(2 * c + 1, 2 * c + 4) for c in range(chips - 2)]
    far += [(2 * c, 2 * c - 3) for c in range(2, chips)] + [(n - 1, n - 3), (n - 3, n - 1)]
    return swap, step, far


def back(pairs):
    return [(b, a) for a, b in pairs]


def shards(queries, key_heads, value_heads, out_grad, doc_lengths, block_reach):
    n = lax.axis_size("seq")
    me = lax.axis_index("seq")
    core = me % 2
    odd = core == 1
    swap, step, far = routes(n)
    send = lambda x, pairs: lax.ppermute(x, "seq", pairs)
    f32 = jnp.float32
    low, high = me, 2 * n - 1 - me
    info = jnp.stack([1 - core, core, jnp.where(odd, low, high), jnp.where(odd, high, low)])

    own = jnp.stack([key_heads[0], value_heads[0]])
    sib = send(own, swap)
    pick = lambda x, c: jnp.where(c, x[:, 1], x[:, 0])
    edge_pair = jnp.stack([pick(own, odd), pick(sib, odd)], axis=1)
    sib_inner = pick(sib, ~odd)[:, None]
    third = send(pick(own, ~odd)[:, None], far)
    r1 = send(edge_pair, step)
    r2 = send(r1, swap)

    att, dq, inner_far, inner_near = attend(
        0, info, doc_lengths, block_reach, queries, out_grad,
        [(r2, 0), (r2, 1), (sib_inner, 0), (own, None)])
    got = send(inner_far, swap)
    att, dq, edge_far, edge_near = attend(
        1, info, doc_lengths, block_reach, queries, out_grad,
        [(third, 0), (r1, 0), (r1, 1), (own, None)], att, dq)

    third_back = send(edge_far[:, :1], back(far))
    both = (edge_far[:, 1:].astype(f32) + got[:, :2].astype(f32)).astype(jnp.bfloat16)
    r1_back = send(both, back(step))
    rest = send(r1_back[:, 1:], swap)
    edge_total = edge_near + got[:, 2].astype(f32) + r1_back[:, 0].astype(f32)
    inner_total = inner_near + third_back[:, 0].astype(f32) + rest[:, 0].astype(f32)
    total = jnp.stack([jnp.where(odd, inner_total, edge_total),
                       jnp.where(odd, edge_total, inner_total)], axis=1).astype(jnp.bfloat16)
    return att, dq, total[0][None], total[1][None]


def solution(mesh):
    wide = P(("dp", "seq"), None, None, None)
    return jax.shard_map(
        shards,
        mesh=mesh,
        in_specs=(wide, wide, wide, wide, P("dp"), P("dp")),
        out_specs=(wide, wide, wide, wide),
        check_vma=False,
    )
```
